32 devices in a mesh: side: 2 (over core), group: 8 (over z, y), head: 2 (over x).
Axes of the slice: x: 2, y: 2, z: 4, core: 2. Of those that a mesh axis runs over, the one named last changes fastest.
Arguments:
- pool_rows: bfloat16 [2, 768, 4096], P('side', ('group', 'head')), may hold values from -24 to 24
- pool_weight: bfloat16 [2, 4096, 8192], P('side', 'group', 'head'), as said below
- lengths: int32 [8, 3], replicated, may hold values from 1 to 48, 96 in all within a row
- owner: int32 [8, 3], replicated, may hold values from 0 to 7, as said below
Outputs:
- pool_out: bfloat16 [2, 768, 4096], P('side', 'group', 'head')
The draws below stay inside these ranges and needn't reach their ends.
Inputs may be any that keep to these rules, and one draw needn't show every extreme that they name: owner[p, j] is p with the binary digits of m_j flipped, where m_j = owner[0, j] is the same for every p; the m_j differ between slots, and every binary digit below 8 is set in some m_j. So the 3 requests of a prefill group go to different decode groups, and every decode group receives exactly one request for each slot j. `lengths`: each row sums to 96. `pool_weight`: independent normal entries of deviation 1 / sqrt(4096).
All inputs are finite; a program needn't handle non-finite values.
Results may differ from the reference program's by a relative error of at most 0.0061.
Values may be sent and summed in bfloat16 or wider, within the bound.
A program may use at most 128 MiB of HBM per device.

```python
import math
import jax
import jax.numpy as jnp
import numpy as np
from jax import lax

D = 4096
HEADS = 16
HEAD_DIM = 256
ROWS_DEV = 48
REQ_G = 3
MEM_G = 96
MAXLEN = 48
TOK = 768
N_GROUP = 8
N_HEAD = 2


def weight_table(key):
    return jax.random.normal(jax.random.fold_in(key, 41), (2, D, 2 * D), jnp.float32) * D ** (-0.5)


def draw_pool_weight(key, part):
    return weight_table(key).astype(jnp.bfloat16)


def draw_pool_rows(key, part):
    noise = jnp.clip(jax.random.normal(jax.random.fold_in(key, 7), (2, TOK, D), jnp.float32), -6.0, 6.0)
    return noise.astype(jnp.bfloat16)


def draw_owner(key, part):
    half = N_GROUP // 2
    other = jax.random.randint(jax.random.fold_in(key, 17), (1,), 0, N_GROUP - 2).astype(jnp.int32)
    other = jnp.where(other >= half, other + 1, other).astype(jnp.int32)
    fixed = jnp.array([half, N_GROUP - 1], jnp.int32)
    flips = jnp.concatenate([fixed, other], axis=0)[:REQ_G]
    order = jax.random.permutation(jax.random.fold_in(key, 29), REQ_G)
    flips = flips[order].astype(jnp.int32)
    groups = jnp.arange(N_GROUP, dtype=jnp.int32)
    return jnp.bitwise_xor(groups[:, None], flips[None, :]).astype(jnp.int32)


def profile(amount, total, reach, slope):
    portions = [(1 << 20) // math.isqrt(grade ** slope) + 1 for grade in range(2, amount + 1)]
    rest, counts = total - reach - (amount - 1), [1] * (amount - 1)
    while rest > 0:
        candidates = [i for i in range(amount - 1) if counts[i] < reach]
        whole, budget = sum([portions[i] for i in candidates]), rest
        for i in candidates:
            extra = min(reach - counts[i], max(1, budget * portions[i] // whole), rest)
            counts[i] = counts[i] + extra
            rest = rest - extra
    return np.array([reach] + counts)


def uneven(key, count, total, reach, lean):
    if count == 2:
        one = jax.random.randint(key, (), max(1, total - reach), min(reach, total - 1) + 1)
        return jnp.stack([one, total - one])
    tallies = jnp.asarray(profile(count, total, reach, lean), jnp.int32)
    twos = (count - 1) // 2
    source_of, receiver = tallies[1:1 + 2 * twos:2], tallies[2:2 + 2 * twos:2]
    slack = jnp.minimum(source_of - 1, reach - receiver)
    moved = jax.random.randint(jax.random.fold_in(key, 1), (twos,), 0, 1 << 20) % (slack + 1)
    tallies = tallies.at[1:1 + 2 * twos:2].set(source_of - moved).at[2:2 + 2 * twos:2].set(receiver + moved)
    return tallies[jax.random.permutation(jax.random.fold_in(key, 2), count)]


def setup_inputs(seed: int = 0) -> dict:
    arg_keys = jax.random.split(jax.random.key(seed), 5)
    pool_rows = draw_pool_rows(jax.random.fold_in(arg_keys[4], 71), 0)
    pool_weight = draw_pool_weight(jax.random.fold_in(arg_keys[4], 71), 0)
    lengths = jax.vmap(lambda own: uneven(own, REQ_G, MEM_G, MAXLEN, 2))(jax.random.split(arg_keys[2], N_GROUP)).reshape((N_GROUP, REQ_G)).astype(jnp.int32)
    owner = draw_owner(jax.random.fold_in(arg_keys[4], 71), 0)
    return dict(pool_rows=pool_rows, pool_weight=pool_weight, lengths=lengths, owner=owner)


def reference(pool_rows, pool_weight, lengths, owner):
    mem_g = ROWS_DEV * N_HEAD
    wide = D // N_HEAD
    q_req = mem_g // REQ_G
    maxlen = mem_g // 2
    scale = 1.0 / (HEAD_DIM ** 0.5)

    def halves(index):
        proj = jnp.dot(pool_rows[index], pool_weight[index], preferred_element_type=jnp.float32)
        proj = proj.reshape(TOK, N_HEAD, 2, wide)
        return proj[:, :, 0, :].reshape(TOK, D), proj[:, :, 1, :].reshape(TOK, D)

    first, second = halves(0)
    keys = first.astype(jnp.bfloat16)
    values = second.astype(jnp.bfloat16)
    queries = halves(1)[0].astype(jnp.bfloat16)
    out_weight = pool_weight[1].reshape(D, N_HEAD, 2, wide)[:, :, 1, :].reshape(D, D)
    starts = jnp.cumsum(lengths, axis=1).astype(jnp.int32) - lengths
    padding = jnp.zeros((maxlen, D), jnp.bfloat16)
    keys_pad = jnp.concatenate([keys, padding], axis=0)
    values_pad = jnp.concatenate([values, padding], axis=0)
    groups = jnp.arange(N_GROUP, dtype=jnp.int32)

    def one_group(decode):
        pieces = []
        for slot in range(REQ_G):
            hit = owner[:, slot] == decode
            source = jnp.sum(jnp.where(hit, groups, 0)).astype(jnp.int32)
            begin = jnp.sum(jnp.where(hit, starts[:, slot], 0)).astype(jnp.int32)
            count = jnp.sum(jnp.where(hit, lengths[:, slot], 0)).astype(jnp.int32)
            first_row = (source * mem_g + begin).astype(jnp.int32)
            key_rows = lax.dynamic_slice_in_dim(keys_pad, first_row, maxlen, 0).reshape(maxlen, HEADS, HEAD_DIM)
            value_rows = lax.dynamic_slice_in_dim(values_pad, first_row, maxlen, 0).reshape(maxlen, HEADS, HEAD_DIM)
            query_start = (decode * mem_g + slot * q_req).astype(jnp.int32)
            query_rows = lax.dynamic_slice_in_dim(queries, query_start, q_req, 0).reshape(q_req, HEADS, HEAD_DIM)
            scores = jnp.einsum("qeh,keh->eqk", query_rows.astype(jnp.float32), key_rows.astype(jnp.float32)) * scale
            valid = jnp.arange(maxlen, dtype=jnp.int32) < count
            scores = jnp.where(valid[None, None, :], scores, -1e30)
            peak = jnp.max(scores, axis=-1, keepdims=True)
            expo = jnp.where(valid[None, None, :], jnp.exp(scores - peak), 0.0)
            total = jnp.sum(expo, axis=-1)
            probs = expo.astype(jnp.bfloat16)
            mixed = jnp.einsum("eqk,keh->eqh", probs.astype(jnp.float32), value_rows.astype(jnp.float32))
            mixed = mixed / total[:, :, None]
            pieces.append(jnp.transpose(mixed, (1, 0, 2)).reshape(q_req, D))
        return jnp.concatenate(pieces, axis=0).astype(jnp.bfloat16)

    attended = lax.map(one_group, groups).reshape(TOK, D)
    decoded = lax.dot_general(attended, out_weight, (((1,), (1,)), ((), ())), preferred_element_type=jnp.float32)
    return jnp.stack([keys, decoded.astype(jnp.bfloat16)], axis=0)
```

```python
import functools

import jax
import jax.numpy as jnp
from jax import lax
from jax.experimental import pallas as pl
from jax.experimental.pallas import tpu as pltpu
from jax.sharding import PartitionSpec as P

HEAD_DIM = 256
LAG = 2
LANES = 128
BF = jnp.bfloat16
F32 = jnp.float32


def low_digit(groups):
    low = 1
    while low * low * 4 <= groups:
        low *= 2
    return low


def aligned(index, size):
    return pl.ds(pl.multiple_of(index * size, size), size)


def kernel(dims, pick_ref, mask_ref, x_ref, w_hbm, out_ref, w, xg, xp, part, ysend, yrecv, zown, zsend, zrecv,
           proj, kv, attg, pout, osend, orecv, wsem, lsem, xss, xrs, fss, frs, yss, yrs, zss, zrs, kss, krs,
           ass, ars, bss, brs, oss, ors):
    ng, nh, nl, nz, rows, mem, kc, wide, ch, req = dims
    nc = wide // ch
    q_req = mem // req
    side = lax.axis_index("side")
    g = lax.axis_index("group")
    h = lax.axis_index("head")
    z = g // nl
    y = g % nl
    scale = 1.0 / HEAD_DIM**0.5

    def remote(src, dst, ssem, rsem, to):
        return pltpu.make_async_remote_copy(
            src_ref=src, dst_ref=dst, send_sem=ssem, recv_sem=rsem, device_id=to,
            device_id_type=pl.DeviceIdType.MESH)

    load_w = pltpu.make_async_copy(w_hbm.at[0], w, wsem)
    load_w.start()

    barrier = pltpu.get_barrier_semaphore()
    others = ng * nh - 1
    me = g * nh + h

    def greet(k, carry):
        to = (me + 1 + k) % (ng * nh)
        pl.semaphore_signal(barrier, inc=1, device_id=(side, to // nh, to % nh), device_id_type=pl.DeviceIdType.MESH)
        return carry

    lax.fori_loop(0, others, greet, 0)
    pl.semaphore_signal(barrier, inc=1, device_id=(1 - side, g, h), device_id_type=pl.DeviceIdType.MESH)
    pl.semaphore_wait(barrier, others + 1)

    def row_slot(gg, hh):
        return aligned(gg * nh + hh, rows)

    own_cols = x_ref.at[:, aligned(g, kc)]
    place = pltpu.make_async_copy(own_cols, xg.at[row_slot(g, h)], lsem)
    place.start()

    def x_send(k):
        to = (g + k) % ng
        return remote(x_ref.at[:, aligned(to, kc)], xg.at[row_slot(g, h)], xss.at[k], xrs.at[k], (side, to, h))

    def x_forward(k, j):
        source = (g - k + ng) % ng
        src = own_cols if k == 0 else xg.at[row_slot(source, h)]
        return remote(src, xg.at[row_slot(source, h)], fss.at[k, j], frs.at[k, j], (side, g, (h + j) % nh))

    for k in range(1, ng):
        x_send(k).start()
    for j in range(1, nh):
        x_forward(0, j).start()
    for k in range(1, ng):
        x_send(k).wait_recv()
        for j in range(1, nh):
            x_forward(k, j).start()
    place.wait()
    for k in range(ng):
        for j in range(1, nh):
            x_forward(k, j).wait_recv()

    def chosen(source_ref, group, slot):
        total = None
        for source in range(ng):
            keep = jnp.broadcast_to(pick_ref[group * req + slot, source:source + 1, :], (q_req, LANES)).astype(BF)
            keep = jnp.concatenate([keep] * (kc // LANES), axis=1)
            term = source_ref[aligned(source * req + slot, q_req), :].astype(BF) * keep
            total = term if total is None else total + term
        return total

    def order(block, carry):
        at, slot = block // req, block % req
        group = (at % nz) * nl + at // nz

        @pl.when(side == 1)
        def _():
            xp[aligned(block, q_req), :] = chosen(xg, group, slot)

        @pl.when(side == 0)
        def _():
            xp[aligned(block, q_req), :] = xg[aligned(group * req + slot, q_req), :]

        return carry

    lax.fori_loop(0, ng * req, order, 0)
    load_w.wait()

    half = nz * mem

    def y_copy(c, k):
        to = z * nl + (y + k) % nl
        return remote(ysend.at[c, k - 1], yrecv.at[c, k - 1], yss.at[c, k - 1], yrs.at[c, k - 1], (side, to, h))

    def z_copy(c, k):
        to = ((z + k) % nz) * nl + y
        return remote(zsend.at[c, k - 1], zrecv.at[c, k - 1], zss.at[c, k - 1], zrs.at[c, k - 1], (side, to, h))

    def kv_copy(c):
        return remote(proj.at[c], kv.at[c], kss.at[c], krs.at[c], (1 - side, g, h))

    chunks = jnp.where(side == 0, 2 * nc, nc)

    def product(c, carry):
        col = jnp.where(side == 0, (c % 2) * nc + c // 2, c)
        block = w[:, aligned(col, ch)]
        for k in range(1, nl):
            got = jnp.dot(xp[aligned((y + k) % nl, half), :], block, preferred_element_type=F32)
            ysend[c, k - 1] = got.astype(BF)
            y_copy(c, k).start()
        part[c] = jnp.dot(xp[aligned(y, half), :], block, preferred_element_type=F32)
        return carry

    lax.fori_loop(0, chunks, product, 0)

    def reduce_y(c):
        for k in range(1, nl):
            y_copy(c, k).wait_recv()
        for k in list(range(1, nz)) + [0]:
            sel = aligned((z + k) % nz, mem)
            total = part[c, sel, :]
            for kk in range(1, nl):
                total = total + yrecv[c, kk - 1, sel, :].astype(F32)
            if k:
                zsend[c, k - 1] = total.astype(BF)
                z_copy(c, k).start()
            else:
                zown[c] = total

    def reduce_z(c):
        total = zown[c]
        for k in range(1, nz):
            z_copy(c, k).wait_recv()
            total = total + zrecv[c, k - 1].astype(F32)
        proj[c] = total.astype(BF)

        @pl.when(side == 0)
        def _():
            kv_copy(c).start()

            @pl.when(c % 2 == 0)
            def _():
                out_ref[:, aligned(c // 2, ch)] = proj[c]

    def reduce(i, carry):
        @pl.when(i < chunks)
        def _():
            reduce_y(i)

        @pl.when(i >= LAG)
        def _():
            reduce_z(i - LAG)

        return carry

    lax.fori_loop(0, chunks + LAG, reduce, 0)

    def az_copy(c, k):
        to = ((z + k) % nz) * nl + y
        here = attg.at[c, aligned(g, mem)]
        return remote(here, here, ass.at[c, k], ars.at[c, k], (side, to, h))

    def ay_copy(c, k, j):
        source = ((z - k + nz) % nz) * nl + y
        here = attg.at[c, aligned(source, mem)]
        return remote(here, here, bss.at[c, k, j], brs.at[c, k, j], (side, z * nl + (y + j) % nl, h))

    def attend(c):
        for b in range(2):
            remote(proj.at[2 * c + b], kv.at[2 * c + b], kss.at[2 * c + b], krs.at[2 * c + b],
                   (1 - side, g, h)).wait_recv()
        allowed = mask_ref[...] == 1
        for e in range(ch // HEAD_DIM):
            cols = slice(e * HEAD_DIM, (e + 1) * HEAD_DIM)
            scores = lax.dot_general(proj[c, :, cols], kv[2 * c, :, cols], (((1,), (1,)), ((), ())),
                                     preferred_element_type=F32) * scale
            scores = jnp.where(allowed, scores, -1e30)
            peak = jnp.max(scores, axis=-1, keepdims=True)
            expo = jnp.where(allowed, jnp.exp(scores - peak), 0.0)
            total = jnp.sum(expo, axis=-1, keepdims=True)
            mixed = jnp.dot(expo.astype(BF), kv[2 * c + 1, :, cols], preferred_element_type=F32) / total
            attg[c, aligned(g, mem), cols] = mixed.astype(BF)
        for k in range(1, nz):
            az_copy(c, k).start()
        for j in range(1, nl):
            ay_copy(c, 0, j).start()

    def forward(c):
        for k in range(1, nz):
            az_copy(c, k).wait_recv()
            for j in range(1, nl):
                ay_copy(c, k, j).start()

    def out_product(c):
        for k in range(nz):
            for j in range(1, nl):
                ay_copy(c, k, j).wait_recv()
        block = w[:, aligned(nc + c, ch)]

        def rows_part(i, carry):
            sel = aligned(i, half)
            got = lax.dot_general(attg[c, sel, :], block, (((1,), (1,)), ((), ())), preferred_element_type=F32)
            pout[sel, :] = jnp.where(c == 0, got, pout[sel, :] + got)
            return carry

        lax.fori_loop(0, nl, rows_part, 0)

    per_head = ng // nh
    home = g // per_head
    slot_here = (g % per_head) * nh + h

    def o_copy(k):
        to = (g + k) % ng
        return remote(osend.at[k], orecv.at[slot_here], oss.at[k], ors.at[slot_here], (side, to, home))

    own_out = pltpu.make_async_copy(osend.at[0], orecv.at[slot_here], ors.at[slot_here])

    @pl.when(side == 1)
    def _():
        pout[...] = jnp.zeros_like(pout)

        def step(i, carry):
            @pl.when(i < nc)
            def _():
                attend(i)

            @pl.when((i >= 1) & (i <= nc))
            def _():
                forward(i - 1)

            @pl.when(i >= 2)
            def _():
                out_product(i - 2)

            return carry

        lax.fori_loop(0, nc + 2, step, 0)

        for k in list(range(1, ng)) + [0]:
            to = (g + k) % ng
            for slot in range(req):
                osend[k, slot * q_req:(slot + 1) * q_req, :] = chosen(pout, to, slot)
            if k:
                o_copy(k).start()
            else:
                @pl.when(h == home)
                def _():
                    own_out.start()

                @pl.when(h != home)
                def _():
                    o_copy(0).start()
        for f in range(per_head):
            total = None
            for hh in range(nh):
                at = f * nh + hh
                pltpu.make_async_copy(osend.at[0], orecv.at[at], ors.at[at]).wait()
                term = orecv[at].astype(F32)
                total = term if total is None else total + term
            out_ref[:, f * kc:(f + 1) * kc] = total.astype(BF)

    for k in range(1, ng):
        x_send(k).wait_send()
    for k in range(ng):
        for j in range(1, nh):
            x_forward(k, j).wait_send()

    def drain(c, carry):
        for k in range(1, nl):
            y_copy(c, k).wait_send()
        for k in range(1, nz):
            z_copy(c, k).wait_send()

        @pl.when(side == 0)
        def _():
            kv_copy(c).wait_send()

        return carry

    lax.fori_loop(0, chunks, drain, 0)

    @pl.when(side == 1)
    def _():
        def drain_out(c, carry):
            for k in range(1, nz):
                az_copy(c, k).wait_send()
            for k in range(nz):
                for j in range(1, nl):
                    ay_copy(c, k, j).wait_send()
            return carry

        lax.fori_loop(0, nc, drain_out, 0)
        for k in range(1, ng):
            o_copy(k).wait_send()

        @pl.when(h != home)
        def _():
            o_copy(0).wait_send()


def on_device(pool_rows, pool_weight, lengths, owner):
    ng, nh = lax.axis_size("group"), lax.axis_size("head")
    nl = low_digit(ng)
    nz = ng // nl
    rows, depth = pool_rows.shape[1:]
    mem = rows * nh
    kc = pool_weight.shape[1]
    wide = pool_weight.shape[2] // 2
    ch = 2 * HEAD_DIM if wide % (2 * HEAD_DIM) == 0 else HEAD_DIM
    nc = wide // ch
    req = lengths.shape[1]
    total = mem * ng
    dims = (ng, nh, nl, nz, rows, mem, kc, wide, ch, req)
    pick = owner.reshape(ng * req, 1) == jnp.arange(ng, dtype=jnp.int32)[None, :]
    pick = jnp.broadcast_to(pick[:, :, None], (ng * req, ng, LANES)).astype(F32)
    count = lax.dynamic_index_in_dim(lengths, lax.axis_index("group"), 0, keepdims=False)
    row_slot = jnp.arange(mem, dtype=jnp.int32)[:, None] // (mem // req)
    key = jnp.arange(mem, dtype=jnp.int32)[None, :]
    mask = jnp.zeros((mem, mem), jnp.int32)
    first = jnp.int32(0)
    for slot in range(req):
        mask = jnp.where((row_slot == slot) & (key >= first) & (key < first + count[slot]), 1, mask)
        first = first + count[slot]
    dma = pltpu.SemaphoreType.DMA
    ly, lz = max(nl - 1, 1), max(nz - 1, 1)
    out = pl.pallas_call(
        functools.partial(kernel, dims),
        out_shape=jax.ShapeDtypeStruct((mem, wide), BF),
        in_specs=[
            pl.BlockSpec(memory_space=pltpu.VMEM),
            pl.BlockSpec(memory_space=pltpu.VMEM),
            pl.BlockSpec(memory_space=pltpu.VMEM),
            pl.BlockSpec(memory_space=pl.ANY),
        ],
        out_specs=pl.BlockSpec(memory_space=pltpu.VMEM),
        scratch_shapes=[
            pltpu.VMEM((kc, 2 * wide), BF),
            pltpu.VMEM((total, kc), BF),
            pltpu.VMEM((total, kc), BF),
            pltpu.VMEM((2 * nc, nz * mem, ch), F32),
            pltpu.VMEM((2 * nc, ly, nz * mem, ch), BF),
            pltpu.VMEM((2 * nc, ly, nz * mem, ch), BF),
            pltpu.VMEM((2 * nc, mem, ch), F32),
            pltpu.VMEM((2 * nc, lz, mem, ch), BF),
            pltpu.VMEM((2 * nc, lz, mem, ch), BF),
            pltpu.VMEM((2 * nc, mem, ch), BF),
            pltpu.VMEM((2 * nc, mem, ch), BF),
            pltpu.VMEM((nc, total, ch), BF),
            pltpu.VMEM((total, kc), F32),
            pltpu.VMEM((ng, mem, kc), BF),
            pltpu.VMEM((ng, mem, kc), BF),
            dma, dma, dma((ng,)), dma((ng,)), dma((ng, nh)), dma((ng, nh)),
            dma((2 * nc, ly)), dma((2 * nc, ly)), dma((2 * nc, lz)), dma((2 * nc, lz)),
            dma((2 * nc,)), dma((2 * nc,)),
            dma((nc, nz)), dma((nc, nz)), dma((nc, nz, nl)), dma((nc, nz, nl)),
            dma((ng,)), dma((ng,)),
        ],
        compiler_params=pltpu.CompilerParams(
            collective_id=0, has_side_effects=True, vmem_limit_bytes=67043328),
    )(pick, mask, pool_rows[0], pool_weight)
    return out[None]


def solution(mesh):
    placed = (P("side", ("group", "head"), None), P("side", "group", "head"), P(), P())
    return jax.shard_map(
        on_device, mesh=mesh, in_specs=placed, out_specs=P("side", "group", "head"), check_vma=False
    )
```

```python
import functools

import jax
import jax.numpy as jnp
from jax import lax
from jax.experimental import pallas as pl
from jax.experimental.pallas import tpu as pltpu
from jax.sharding import PartitionSpec as P

HEAD_DIM = 256
LAG = 1
EARLY = 2
CELL = 4
LANES = 128
BF = jnp.bfloat16
F32 = jnp.float32
MESH = pl.DeviceIdType.MESH


def aligned(index, size):
    return pl.ds(pl.multiple_of(index * size, size), size)


def kernel(dims, owner_ref, lengths_ref, x_ref, w_hbm, out_ref, ow, wv, xg, prod, zown, zsend, zrecv, proj, kv, kx,
           attg, pout, osend, omid, orecv, osem, wss, wrs, xss, xrs, lss, lrs, hss, hrs, zss, zrs, kss, krs,
           yss, yrs, ass, ars, bss, brs, oss, ors, pss, prs):
    ng, nh, nl, nz, rows, mem, kc, wide, ch, req = dims
    part = wide // nl
    nc = part // ch
    q_req = mem // req
    cell = nl * mem
    depth = nl * kc
    side = lax.axis_index("side")
    g = lax.axis_index("group")
    h = lax.axis_index("head")
    z = g // nl
    lo = g % nl
    scale = 1.0 / HEAD_DIM**0.5
    chunks = jnp.where(side == 0, 2 * nc, nc)

    def remote(src, dst, ssem, rsem, to):
        return pltpu.make_async_remote_copy(
            src_ref=src, dst_ref=dst, send_sem=ssem, recv_sem=rsem, device_id=to, device_id_type=MESH)

    def at(zz, ll):
        return (side, ((zz + nz) % nz) * nl + (ll + nl) % nl, h)

    def w_cols(i, ll):
        second = jnp.where(side == 0, i % 2, 0)
        step = jnp.where(side == 0, i // 2, i)
        return aligned(second * (wide // ch) + ll * nc + step, ch)

    def w_copy(i, k):
        to = (lo + k) % nl
        return remote(w_hbm.at[0, :, w_cols(i, to)], wv.at[i, aligned(lo, kc)], wss.at[i, k], wrs.at[i, k], at(z, to))

    def w_own(i):
        return pltpu.make_async_copy(w_hbm.at[0, :, w_cols(i, lo)], wv.at[i, aligned(lo, kc)], wrs.at[i, 0])

    load_out = pltpu.make_async_copy(w_hbm.at[0, :, pl.ds(wide, wide)], ow, osem)

    def load_own(i, carry):
        w_own(i).start()
        return carry

    lax.fori_loop(0, chunks, load_own, 0)

    @pl.when(side == 1)
    def _():
        load_out.start()

    barrier = pltpu.get_barrier_semaphore()
    others = ng * nh - 1
    me = g * nh + h

    def greet(k, carry):
        to = (me + 1 + k) % (ng * nh)
        pl.semaphore_signal(barrier, inc=1, device_id=(side, to // nh, to % nh), device_id_type=MESH)
        return carry

    lax.fori_loop(0, others, greet, 0)
    pl.semaphore_signal(barrier, inc=1, device_id=(1 - side, g, h), device_id_type=MESH)
    pl.semaphore_wait(barrier, others + 1)

    def start_w(i, carry):
        for k in range(1, nl):
            w_copy(i, k).start()
        return carry

    def row_slot(gg, hh):
        return aligned(gg * nh + hh, rows)

    own_cols = x_ref.at[0, :, aligned(z, depth)]
    place = pltpu.make_async_copy(own_cols, xg.at[row_slot(g, h)], xrs.at[0])
    place.start()

    def x_high(k):
        to = (z + k) % nz
        return remote(x_ref.at[0, :, aligned(to, depth)], xg.at[row_slot(g, h)], xss.at[k], xrs.at[k], at(to, lo))

    def block_of(k, j):
        source = ((z - k + nz) % nz) * nl + (lo - j + nl) % nl
        dst = xg.at[row_slot(source, h)]
        return (own_cols if k == 0 and j == 0 else dst), dst

    def x_low(k, j):
        src, dst = block_of(k, 0)
        return remote(src, dst, lss.at[k, j], lrs.at[k, j], at(z, lo + j))

    def x_head(k, j, m):
        src, dst = block_of(k, j)
        return remote(src, dst, hss.at[k, j, m], hrs.at[k, j, m], (side, g, (h + m) % nh))

    for k in range(1, nz):
        x_high(k).start()
    for k in range(nz):
        if k:
            x_high(k).wait_recv()
        for j in range(1, nl):
            x_low(k, j).start()
        for m in range(1, nh):
            x_head(k, 0, m).start()
    lax.fori_loop(0, jnp.minimum(EARLY, chunks), start_w, 0)
    for k in range(nz):
        for j in range(1, nl):
            x_low(k, j).wait_recv()
            for m in range(1, nh):
                x_head(k, j, m).start()
    lax.fori_loop(jnp.minimum(EARLY, chunks), chunks, start_w, 0)
    place.wait()
    for k in range(nz):
        for j in range(nl):
            for m in range(1, nh):
                x_head(k, j, m).wait_recv()

    def chosen(source_ref, group, slot, lanes):
        which = jnp.broadcast_to(owner_ref[pl.ds(group, 1), slot:slot + 1], (q_req, LANES))
        total = jnp.zeros((q_req, LANES), F32)
        for source in range(ng):
            start = (source * req + slot) * q_req
            total = jnp.where(which == source, source_ref[start:start + q_req, lanes], total)
        return total

    def z_copy(c, k):
        return remote(zsend.at[c, k - 1], zrecv.at[c, k - 1], zss.at[c, k - 1], zrs.at[c, k - 1], at(z + k, lo))

    def kv_copy(c):
        return remote(proj.at[c], kv.at[c], kss.at[c], krs.at[c], (1 - side, g, h))

    def key_copy(c, k):
        to = (lo + k) % nl
        return remote(proj.at[2 * c, aligned(to, mem)], kx.at[c, lo], yss.at[c, k], yrs.at[c, k], at(z, to))

    def product(c):
        w_own(c).wait()
        for k in range(1, nl):
            w_copy(c, k).wait_recv()

        def rows_part(i, carry):
            sel = aligned(i, cell)
            prod[sel, :] = jnp.dot(xg[sel, :], wv[c], preferred_element_type=F32)
            return carry

        lax.fori_loop(0, nz, rows_part, 0)
        for k in list(range(1, nz)) + [0]:
            to = (z + k) % nz

            @pl.when(side == 0)
            def _():
                if k:
                    zsend[c, k - 1] = prod[aligned(to, cell), :].astype(BF)
                else:
                    zown[c] = prod[aligned(to, cell), :]

            @pl.when(side == 1)
            def _():
                def member(ll, carry):
                    for slot in range(req):
                        put = aligned(ll * req + slot, q_req)
                        for lane in range(ch // LANES):
                            lanes = slice(lane * LANES, (lane + 1) * LANES)
                            got = chosen(prod, to * nl + ll, slot, lanes)
                            if k:
                                zsend[c, k - 1, put, lanes] = got.astype(BF)
                            else:
                                zown[c, put, lanes] = got
                    return carry

                lax.fori_loop(0, nl, member, 0)

            if k:
                z_copy(c, k).start()

    def reduce_z(c):
        total = zown[c]
        for k in range(1, nz):
            z_copy(c, k).wait_recv()
            total = total + zrecv[c, k - 1].astype(F32)
        proj[c] = total.astype(BF)

        @pl.when(side == 0)
        def _():
            kv_copy(c).start()

            @pl.when(c % 2 == 0)
            def _():
                for k in range(1, nl):
                    key_copy(c // 2, k).start()
                out_ref[:, aligned(lo * nc + c // 2, ch)] = proj[c, aligned(lo, mem), :]

    def reduce(i, carry):
        @pl.when(i < chunks)
        def _():
            product(i)

        @pl.when(i >= LAG)
        def _():
            reduce_z(i - LAG)

        return carry

    lax.fori_loop(0, chunks + LAG, reduce, 0)

    def az_copy(c, k):
        here = attg.at[lo * nc + c, aligned(z, cell)]
        return remote(here, here, ass.at[c, k], ars.at[c, k], at(z + k, lo))

    def ay_copy(c, k, j):
        here = attg.at[lo * nc + c, aligned((z - k + nz) % nz, cell)]
        return remote(here, here, bss.at[c, k, j], brs.at[c, k, j], at(z, lo + j))

    def allowed_keys():
        row = lax.broadcasted_iota(jnp.int32, (cell, cell), 0)
        key = lax.broadcasted_iota(jnp.int32, (cell, cell), 1)
        slots = row // q_req
        lower = jnp.zeros((cell, cell), jnp.int32)
        upper = jnp.zeros((cell, cell), jnp.int32)
        for ll in range(nl):
            first = jnp.full((1, 1), ll * mem, jnp.int32)
            for slot in range(req):
                here = slots == ll * req + slot
                last = first + lengths_ref[pl.ds(z * nl + ll, 1), slot:slot + 1]
                lower = jnp.where(here, jnp.broadcast_to(first, (cell, cell)), lower)
                upper = jnp.where(here, jnp.broadcast_to(last, (cell, cell)), upper)
                first = last
        return (key >= lower) & (key < upper)

    def attend(c):
        for b in range(2):
            kv_copy(2 * c + b).wait_recv()
        allowed = allowed_keys()
        for e in range(ch // HEAD_DIM):
            cols = slice(e * HEAD_DIM, (e + 1) * HEAD_DIM)
            scores = lax.dot_general(proj[c, :, cols], kv[2 * c, :, cols], (((1,), (1,)), ((), ())),
                                     preferred_element_type=F32) * scale
            scores = jnp.where(allowed, scores, -1e30)
            peak = jnp.max(scores, axis=-1, keepdims=True)
            expo = jnp.where(allowed, jnp.exp(scores - peak), 0.0)
            total = jnp.sum(expo, axis=-1, keepdims=True)
            mixed = jnp.dot(expo.astype(BF), kv[2 * c + 1, :, cols], preferred_element_type=F32) / total
            attg[lo * nc + c, aligned(z, cell), cols] = mixed.astype(BF)
        for k in range(1, nz):
            az_copy(c, k).start()
        for j in range(1, nl):
            ay_copy(c, 0, j).start()

    def forward(c):
        for k in range(1, nz):
            az_copy(c, k).wait_recv()
            for j in range(1, nl):
                ay_copy(c, k, j).start()

    def out_product(c):
        for j in range(nl):
            if j:
                for k in range(nz):
                    ay_copy(c, k, j).wait_recv()
            index = ((lo - j + nl) % nl) * nc + c
            block = ow[:, aligned(index, ch)]

            def rows_part(i, carry):
                sel = aligned(i, cell)
                got = lax.dot_general(attg[index, sel, :], block, (((1,), (1,)), ((), ())),
                                      preferred_element_type=F32)
                pout[sel, :] = pout[sel, :] + got
                return carry

            lax.fori_loop(0, nz, rows_part, 0)

    per_head = ng // nh

    def o_copy(k):
        to = (g + k) % ng
        return remote(osend.at[k], omid.at[g], oss.at[k], ors.at[k], (side, to, h))

    def o_head(gg):
        slot = (gg % per_head) * nh + h
        return remote(omid.at[gg], orecv.at[slot], pss.at[gg], prs.at[slot], (side, g, gg // per_head))

    @pl.when(side == 1)
    def _():
        pout[...] = jnp.zeros_like(pout)
        load_out.wait()

        def step(i, carry):
            @pl.when(i < nc)
            def _():
                attend(i)

            @pl.when((i >= 1) & (i <= nc))
            def _():
                forward(i - 1)

            @pl.when(i >= 2)
            def _():
                out_product(i - 2)

            return carry

        lax.fori_loop(0, nc + 2, step, 0)

        def spread(i, carry):
            k = (i + 1) % ng
            to = (g + k) % ng
            for slot in range(req):
                for lane in range(kc // LANES):
                    lanes = slice(lane * LANES, (lane + 1) * LANES)
                    osend[k, slot * q_req:(slot + 1) * q_req, lanes] = chosen(pout, to, slot, lanes).astype(BF)

            @pl.when(k > 0)
            def _():
                o_copy(k).start()

            return carry

        lax.fori_loop(0, ng, spread, 0)
        omid[g] = osend[0]

        def pass_on(k, carry):
            gg = (g - k + ng) % ng

            @pl.when(k > 0)
            def _():
                o_copy(k).wait_recv()

            @pl.when(gg // per_head != h)
            def _():
                o_head(gg).start()

            return carry

        lax.fori_loop(0, ng, pass_on, 0)
        for f in range(per_head):
            total = omid[h * per_head + f].astype(F32)
            for m in range(1, nh):
                slot = f * nh + (h + m) % nh
                remote(omid.at[0], orecv.at[slot], pss.at[0], prs.at[slot], (side, g, (h + m) % nh)).wait_recv()
                total = total + orecv[slot].astype(F32)
            out_ref[:, f * kc:(f + 1) * kc] = total.astype(BF)

    @pl.when(side == 0)
    def _():
        for c in range(nc):
            for k in range(1, nl):
                key_copy(c, k).wait_recv()
                source = (lo - k + nl) % nl
                out_ref[:, aligned(source * nc + c, ch)] = kx[c, source]

    for k in range(nz):
        if k:
            x_high(k).wait_send()
        for j in range(nl):
            if j:
                x_low(k, j).wait_send()
            for m in range(1, nh):
                x_head(k, j, m).wait_send()

    def drain(c, carry):
        for k in range(1, nl):
            w_copy(c, k).wait_send()
        for k in range(1, nz):
            z_copy(c, k).wait_send()

        @pl.when(side == 0)
        def _():
            kv_copy(c).wait_send()

        return carry

    lax.fori_loop(0, chunks, drain, 0)

    @pl.when(side == 0)
    def _():
        for c in range(nc):
            for k in range(1, nl):
                key_copy(c, k).wait_send()

    @pl.when(side == 1)
    def _():
        def drain_out(c, carry):
            for k in range(1, nz):
                az_copy(c, k).wait_send()
            for k in range(nz):
                for j in range(1, nl):
                    ay_copy(c, k, j).wait_send()
            return carry

        lax.fori_loop(0, nc, drain_out, 0)

        def drain_last(k, carry):
            gg = (g - k + ng) % ng

            @pl.when(k > 0)
            def _():
                o_copy(k).wait_send()

            @pl.when(gg // per_head != h)
            def _():
                o_head(gg).wait_send()

            return carry

        lax.fori_loop(0, ng, drain_last, 0)


def on_device(pool_rows, pool_weight, lengths, owner):
    ng, nh = lax.axis_size("group"), lax.axis_size("head")
    rows = pool_rows.shape[1]
    mem = rows * nh
    kc = pool_weight.shape[1]
    wide = pool_weight.shape[2] // 2
    nl = min(CELL, wide // HEAD_DIM)
    nz = ng // nl
    ch = HEAD_DIM
    nc = wide // nl // ch
    req = lengths.shape[1]
    total = mem * ng
    cell = nl * mem
    dims = (ng, nh, nl, nz, rows, mem, kc, wide, ch, req)
    dma = pltpu.SemaphoreType.DMA
    lz = max(nz - 1, 1)
    out = pl.pallas_call(
        functools.partial(kernel, dims),
        out_shape=jax.ShapeDtypeStruct((mem, wide), BF),
        in_specs=[
            pl.BlockSpec(memory_space=pltpu.VMEM),
            pl.BlockSpec(memory_space=pltpu.VMEM),
            pl.BlockSpec(memory_space=pltpu.VMEM),
            pl.BlockSpec(memory_space=pl.ANY),
        ],
        out_specs=pl.BlockSpec(memory_space=pltpu.VMEM),
        scratch_shapes=[
            pltpu.VMEM((kc, wide), BF),
            pltpu.VMEM((2 * nc, nl * kc, ch), BF),
            pltpu.VMEM((total, nl * kc), BF),
            pltpu.VMEM((total, ch), F32),
            pltpu.VMEM((2 * nc, cell, ch), F32),
            pltpu.VMEM((2 * nc, lz, cell, ch), BF),
            pltpu.VMEM((2 * nc, lz, cell, ch), BF),
            pltpu.VMEM((2 * nc, cell, ch), BF),
            pltpu.VMEM((2 * nc, cell, ch), BF),
            pltpu.VMEM((nc, nl, mem, ch), BF),
            pltpu.VMEM((nl * nc, total, ch), BF),
            pltpu.VMEM((total, kc), F32),
            pltpu.VMEM((ng, mem, kc), BF),
            pltpu.VMEM((ng, mem, kc), BF),
            pltpu.VMEM((ng, mem, kc), BF),
            dma, dma((2 * nc, nl)), dma((2 * nc, nl)), dma((nz,)), dma((nz,)), dma((nz, nl)), dma((nz, nl)),
            dma((nz, nl, nh)), dma((nz, nl, nh)), dma((2 * nc, lz)), dma((2 * nc, lz)),
            dma((2 * nc,)), dma((2 * nc,)), dma((nc, nl)), dma((nc, nl)),
            dma((nc, nz)), dma((nc, nz)), dma((nc, nz, nl)), dma((nc, nz, nl)),
            dma((ng,)), dma((ng,)), dma((ng,)), dma((ng,)),
        ],
        compiler_params=pltpu.CompilerParams(
            collective_id=0, has_side_effects=True, vmem_limit_bytes=67043328),
    )(owner, lengths, pool_rows, pool_weight)
    return out[None]


def solution(mesh):
    placed = (P("side", ("group", "head"), None), P("side", "group", "head"), P(), P())
    return jax.shard_map(
        on_device, mesh=mesh, in_specs=placed, out_specs=P("side", "group", "head"), check_vma=False
    )
```
